512 devices in a mesh: row: 64 (over z, x, core), col: 8 (over y).
Axes of the slice: x: 4, y: 8, z: 8, core: 2. Of those that a mesh axis runs over, the one named last changes fastest.
Arguments:
- amplitudes: bfloat16 [512, 256, 256], P('col', 'row'), may hold values from -6 to 6
- integrals: bfloat16 [256, 48, 256, 256], P('row', 'col'), may hold values from -0.03125 to 0.03125
- screen: int32 [256, 48], P('row', 'col'), may hold values from -1 to 7, as said below
- owner_map: int32 [8, 8], P('col'), may hold values from 0 to 7, each once within a row
Outputs:
- ladder: float32 [512, 64, 256], P('row', 'col')
The draws below stay inside these ranges and needn't reach their ends.
Inputs may be any that keep to these rules, and one draw needn't show every extreme that they name: `screen`: in each row and column group the 6 slots first name distinct result tiles of that group, then hold -1; at least 2 are live, and some group of some row has all 6 live.
All inputs are finite; a program needn't handle non-finite values.
Results may differ from the reference program's by a relative error of at most 0.0003.
Values may be sent and summed in bfloat16 or wider, within the bound.
A program may use at most 64 MiB of HBM per device.

```python
import jax
import jax.numpy as jnp
from jax import lax

TILE = 256
SLOTS = 6
AB_COL = 8
PAIRS = 512
NCD = 256
NAB = 64
LISTS = 48
N_COL = 8


def draw_screen(key, part):
    count_rows = NCD * N_COL
    keys = jax.random.split(jax.random.fold_in(key, 11), count_rows)
    perms = jax.vmap(lambda single: jax.random.permutation(single, AB_COL))(keys)[:, :SLOTS]
    counts = jax.random.randint(jax.random.fold_in(key, 12), (count_rows,), 2, SLOTS + 1)
    counts = counts.at[0].set(SLOTS)
    position = jnp.arange(SLOTS, dtype=jnp.int32)
    lists = jnp.where(position[None, :] < counts[:, None], perms.astype(jnp.int32), -1)
    return lists.reshape(NCD, N_COL * SLOTS).astype(jnp.int32)


def steps_of(own_key, shape, shards, low, largest):
    gain, own = 1.0, jax.random.fold_in(own_key, 6)
    for axis_at, blocks in shards:
        draws = jnp.exp(jax.random.uniform(jax.random.fold_in(own, axis_at), (blocks,), jnp.float32, low / len(shards), largest / len(shards)))
        gain = gain * jnp.repeat(draws, shape[axis_at] // blocks).reshape([-1 if axis == axis_at else 1 for axis in range(len(shape))])
    return gain


def scatter_about(stream_key, dims, width, most, cuts=(), kind=jnp.bfloat16):
    array = jax.random.normal(stream_key, dims, jnp.float32) * width
    if len(cuts) > 0:
        array = steps_of(stream_key, dims, cuts, -0.22, 0.18) * array
    return jnp.clip(array, min=-most, max=most).astype(kind)


def setup_inputs(seed: int = 0) -> dict:
    seeds = jax.random.split(jax.random.key(seed), 5)
    amplitudes = scatter_about(seeds[0], (PAIRS, NCD, TILE), 1.0, 6.0, ((0, 8), (1, 64)))
    integrals = scatter_about(seeds[1], (NCD, LISTS, TILE, TILE), (NCD * TILE // 2) ** -0.5, 0.03125, ((0, 64), (1, 8)))
    screen = draw_screen(jax.random.fold_in(seeds[4], 71), 0)
    owner_map = jax.vmap(lambda own: jax.random.permutation(own, AB_COL))(jax.random.split(seeds[3], N_COL)).reshape((N_COL, AB_COL)).astype(jnp.int32)
    return {"amplitudes": amplitudes, "integrals": integrals, "screen": screen, "owner_map": owner_map}


def reference(amplitudes, integrals, screen, owner_map):
    lists = screen.reshape(NCD, N_COL, SLOTS)
    live = lists >= 0
    safe = jnp.maximum(lists, 0)
    table = jnp.broadcast_to(owner_map[None, :, :], (NCD, N_COL, AB_COL))
    stored = jnp.take_along_axis(table, safe, axis=2)
    groups = jnp.arange(N_COL, dtype=jnp.int32)[None, :, None] * AB_COL
    target = (stored + groups).reshape(NCD, LISTS)
    livemask = live.reshape(NCD, LISTS)
    columns = jnp.arange(NAB, dtype=jnp.int32)
    onehot = ((target[:, :, None] == columns[None, None, :]) & livemask[:, :, None]).astype(jnp.float32)

    def step(total, index):
        amp_tile = lax.dynamic_index_in_dim(amplitudes, index, 1, keepdims=False).astype(jnp.float32)
        blocks = lax.dynamic_index_in_dim(integrals, index, 0, keepdims=False).astype(jnp.float32)
        select = lax.dynamic_index_in_dim(onehot, index, 0, keepdims=False)
        contrib = jnp.einsum('pw,swv->psv', amp_tile, blocks, precision=lax.Precision.HIGHEST)
        total = total + jnp.einsum('psv,sa->pav', contrib, select, precision=lax.Precision.HIGHEST)
        return total, None

    start = jnp.zeros((PAIRS, NAB, TILE), jnp.float32)
    result, unused = lax.scan(step, start, jnp.arange(NCD, dtype=jnp.int32))
    return result
```

```python
import functools

import jax
import jax.numpy as jnp
from jax import lax
from jax.experimental import pallas as pl
from jax.experimental.pallas import tpu as pltpu
from jax.sharding import PartitionSpec as P

MESH = pl.DeviceIdType.MESH
NX, NZ, NY = 4, 8, 8


def kernel(screen_ref, owner_ref, amp_ref, integrals_ref, out_ref,
           tiles, pick, gath, part, mate, fromx, red, fromz,
           load_sem, y_send, y_recv, c_send, c_recv, x_send, x_recv, z_send, z_recv):
    row, y = lax.axis_index("row"), lax.axis_index("col")
    core = lax.rem(row, 2)
    x = lax.rem(row // 2, NX)
    z = row // (2 * NX)

    def dev(zz, xx, cc):
        return ((zz * NX + xx) * 2 + cc, y)

    right = (row, lax.rem(y + 1, NY))
    left = (row, lax.rem(y + NY - 1, NY))

    load = pltpu.make_async_copy(integrals_ref, tiles.at[pl.ds(0, 24)], load_sem)
    load.start()

    barrier = pltpu.get_barrier_semaphore()
    peers = [right, left, dev(z, x, 1 - core)]
    peers += [dev(z, lax.rem(x + o, NX), core) for o in range(1, NX)]
    peers += [dev(lax.rem(z + o, NZ), x, core) for o in range(1, NZ)]
    for peer in peers:
        pl.semaphore_signal(barrier, inc=1, device_id=peer, device_id_type=MESH)
    pl.semaphore_wait(barrier, len(peers))

    def y_copy(step, d):
        src = amp_ref if step == 1 else gath.at[step - 1, :, d]
        return pltpu.make_async_remote_copy(
            src_ref=src, dst_ref=gath.at[step, :, d],
            send_sem=y_send.at[step, d], recv_sem=y_recv.at[step, d],
            device_id=right if d == 0 else left, device_id_type=MESH)

    def c_copy(slot):
        return pltpu.make_async_remote_copy(
            src_ref=part.at[slot, 1 - core], dst_ref=mate.at[slot],
            send_sem=c_send.at[slot], recv_sem=c_recv.at[slot],
            device_id=dev(z, x, 1 - core), device_id_type=MESH)

    def x_copy(slot, o):
        xx = lax.rem(x + o, NX)
        return pltpu.make_async_remote_copy(
            src_ref=part.at[slot, core, xx], dst_ref=fromx.at[slot, o - 1],
            send_sem=x_send.at[slot, o - 1], recv_sem=x_recv.at[slot, o - 1],
            device_id=dev(z, xx, core), device_id_type=MESH)

    def block_of(slot):
        if slot == 0:
            return y
        s = (slot + 1) // 2
        return lax.rem(y + NY - s, NY) if slot % 2 == 1 else lax.rem(y + s, NY)

    def z_copy(slot):
        return pltpu.make_async_remote_copy(
            src_ref=red.at[slot], dst_ref=fromz.at[z],
            send_sem=z_send.at[slot], recv_sem=z_recv.at[z],
            device_id=dev(block_of(slot), x, core), device_id_type=MESH)

    y_copy(1, 0).start()
    y_copy(1, 1).start()

    tiles[24] = jnp.zeros((256, 256), jnp.bfloat16)
    for t in range(8):
        label = jnp.int32(0)
        for g in range(8):
            label = jnp.where(owner_ref[0, g] == t, g, label)
        for k in range(4):
            at = jnp.int32(24)
            for l in range(6):
                at = jnp.where(screen_ref[k, l] == label, k * 6 + l, at)
            pick[k * 8 + t] = at
    load.wait()

    def product(step):
        single = step == 0 or step == 4
        slots = [0] if step == 0 else ([7] if step == 4 else [2 * step - 1, 2 * step])

        def tile(t, carry):
            total = None
            for k in range(4):
                if step == 0:
                    rows = amp_ref[k]
                elif step == 4:
                    rows = gath[4, k, 0]
                else:
                    rows = gath[step, k].reshape(128, 256)
                term = jnp.dot(rows, tiles[pick[k * 8 + t]], preferred_element_type=jnp.float32)
                total = term if total is None else total + term
            total = total.reshape(len(slots), NX, 2, 8, 256)
            for i, slot in enumerate(slots):
                for xx in range(NX):
                    for cc in range(2):
                        part[slot, cc, xx, t] = total[i, xx, cc]
            return carry

        lax.fori_loop(0, 8, tile, 0)
        for slot in slots:
            c_copy(slot).start()
        return slots

    def join(slots):
        for slot in slots:
            c_copy(slot).wait()

            def add(xx, carry):
                part[slot, core, xx] = part[slot, core, xx] + mate[slot, xx]
                return carry

            lax.fori_loop(0, NX, add, 0)
            for o in (2, 1, 3):
                x_copy(slot, o).start()

    def across(slots):
        for slot in slots:
            for o in range(1, NX):
                x_copy(slot, o).wait()
            total = part[slot, core, x]
            for o in range(1, NX):
                total = total + fromx[slot, o - 1]
            block = block_of(slot)

            @pl.when(block == z)
            def _():
                fromz[z] = total

            @pl.when(block != z)
            def _():
                red[slot] = total
                z_copy(slot).start()

    done = []
    for step in range(5):
        if step >= 1:
            for d in range(2):
                if d == 1 and step == 4:
                    continue
                y_copy(step, d).wait()
                if step + 1 <= 4 - d:
                    y_copy(step + 1, d).start()
        done.append(product(step))
        if step >= 1:
            join(done[step - 1])
        if step >= 2:
            across(done[step - 2])
    join(done[4])
    across(done[3])
    across(done[4])

    for slot in range(8):
        @pl.when(block_of(slot) != z)
        def _():
            z_copy(slot).wait_send()

    total = fromz[z]
    for o in range(1, NZ):
        zz = lax.rem(z + o, NZ)
        pltpu.make_async_remote_copy(
            src_ref=red.at[0], dst_ref=fromz.at[zz],
            send_sem=z_send.at[0], recv_sem=z_recv.at[zz],
            device_id=dev(zz, x, core), device_id_type=MESH).wait_recv()
        total = total + fromz[zz]
    out_ref[...] = total


def body(amplitudes, integrals, screen, owner_map):
    amp = jnp.transpose(amplitudes, (1, 0, 2))
    tiles = integrals.reshape(24, 256, 256)
    f32 = jnp.float32
    dma = pltpu.SemaphoreType.DMA
    out = pl.pallas_call(
        kernel,
        out_shape=jax.ShapeDtypeStruct((8, 8, 256), f32),
        in_specs=[
            pl.BlockSpec(memory_space=pltpu.SMEM),
            pl.BlockSpec(memory_space=pltpu.SMEM),
            pl.BlockSpec(memory_space=pltpu.VMEM),
            pl.BlockSpec(memory_space=pl.ANY),
        ],
        out_specs=pl.BlockSpec(memory_space=pltpu.VMEM),
        scratch_shapes=[
            pltpu.VMEM((25, 256, 256), jnp.bfloat16),
            pltpu.SMEM((32,), jnp.int32),
            pltpu.VMEM((5, 4, 2, 64, 256), jnp.bfloat16),
            pltpu.VMEM((8, 2, NX, 8, 8, 256), f32),
            pltpu.VMEM((8, NX, 8, 8, 256), f32),
            pltpu.VMEM((8, NX - 1, 8, 8, 256), f32),
            pltpu.VMEM((8, 8, 8, 256), f32),
            pltpu.VMEM((8, 8, 8, 256), f32),
            dma(()),
            dma((5, 2)), dma((5, 2)),
            dma((8,)), dma((8,)),
            dma((8, 3)), dma((8, 3)),
            dma((8,)), dma((8,)),
        ],
        compiler_params=pltpu.CompilerParams(collective_id=0, has_side_effects=True),
    )(screen, owner_map, amp, tiles)
    return jnp.transpose(out, (1, 0, 2))


def solution(mesh):
    return jax.shard_map(
        body,
        mesh=mesh,
        in_specs=(
            P("col", "row", None),
            P("row", "col", None, None),
            P("row", "col"),
            P("col", None),
        ),
        out_specs=P("row", "col", None),
        check_vma=False,
    )
```

```python
import jax
import jax.numpy as jnp
from jax import lax
from jax.experimental import pallas as pl
from jax.experimental.pallas import tpu as pltpu
from jax.sharding import PartitionSpec as P

MESH = pl.DeviceIdType.MESH
NX, NZ, NY = 4, 8, 8


def kernel(screen_ref, owner_ref, amp_ref, integrals_ref, out_ref,
           tiles, pick, gath, part, mate, relay, near, red, fromz, last,
           load_sem, y_send, y_recv, c_send, c_recv, x_send, x_recv, z_send, z_recv, l_send, l_recv):
    row, y = lax.axis_index("row"), lax.axis_index("col")
    core = lax.rem(row, 2)
    x = lax.rem(row // 2, NX)
    z = row // (2 * NX)

    def dev(zz, xx, cc):
        return ((zz * NX + xx) * 2 + cc, y)

    right = (row, lax.rem(y + 1, NY))
    left = (row, lax.rem(y + NY - 1, NY))
    xp, xf, xm = (lax.rem(x + o, NX) for o in (1, 2, 3))
    zp, zm = lax.rem(z + 1, NZ), lax.rem(z + NZ - 1, NZ)

    load = pltpu.make_async_copy(integrals_ref, tiles.at[pl.ds(0, 24)], load_sem)
    load.start()

    barrier = pltpu.get_barrier_semaphore()
    peers = [right, left, dev(z, x, 1 - core), dev(z, xp, core), dev(z, xm, core)]
    peers += [dev(lax.rem(z + o, NZ), x, core) for o in range(1, NZ)]
    for peer in peers:
        pl.semaphore_signal(barrier, inc=1, device_id=peer, device_id_type=MESH)
    pl.semaphore_wait(barrier, len(peers))

    def y_copy(step, d, h):
        k = pl.ds(2 * h, 2)
        src = amp_ref.at[k] if step == 1 else gath.at[step - 1, k, d]
        return pltpu.make_async_remote_copy(
            src_ref=src, dst_ref=gath.at[step, k, d],
            send_sem=y_send.at[step, d, h], recv_sem=y_recv.at[step, d, h],
            device_id=right if d == 0 else left, device_id_type=MESH)

    def c_copy(slot):
        return pltpu.make_async_remote_copy(
            src_ref=part.at[slot, 1 - core], dst_ref=mate.at[slot],
            send_sem=c_send.at[slot], recv_sem=c_recv.at[slot],
            device_id=dev(z, x, 1 - core), device_id_type=MESH)

    low, high = pl.ds(0, 4), pl.ds(4, 4)

    def x_copy(slot, i):
        to = xp if i % 2 == 0 else xm
        half = low if i in (0, 3, 4) else high
        piece = xf if i < 2 else to
        dst = relay.at[slot, i] if i < 2 else near.at[slot, i % 2, half]
        return pltpu.make_async_remote_copy(
            src_ref=part.at[slot, core, piece, half], dst_ref=dst,
            send_sem=x_send.at[slot, i], recv_sem=x_recv.at[slot, i],
            device_id=dev(z, to, core), device_id_type=MESH)

    def block_of(slot):
        if slot == 0:
            return y
        s = (slot + 1) // 2
        return lax.rem(y + NY - s, NY) if slot % 2 == 1 else lax.rem(y + s, NY)

    def ahead(slot):
        return lax.rem(block_of(slot) + NZ - z, NZ)

    def z_copy(slot, d, half):
        return pltpu.make_async_remote_copy(
            src_ref=red.at[slot, half], dst_ref=fromz.at[slot, d, half],
            send_sem=z_send.at[slot, d], recv_sem=z_recv.at[slot, d],
            device_id=dev(zp if d == 0 else zm, x, core), device_id_type=MESH)

    whole = pl.ds(0, 8)

    def last_copy(at):
        return pltpu.make_async_remote_copy(
            src_ref=red.at[7], dst_ref=last.at[at],
            send_sem=l_send, recv_sem=l_recv.at[at],
            device_id=dev(block_of(7), x, core), device_id_type=MESH)

    for h in range(2):
        for d in range(2):
            y_copy(1, d, h).start()

    tiles[24] = jnp.zeros((256, 256), jnp.bfloat16)
    for t in range(8):
        label = jnp.int32(0)
        for g in range(8):
            label = jnp.where(owner_ref[0, g] == t, g, label)
        for k in range(4):
            at = jnp.int32(24)
            for l in range(6):
                at = jnp.where(screen_ref[k, l] == label, k * 6 + l, at)
            pick[k * 8 + t] = at
    load.wait()

    groups = [[0], [1, 2], [3, 4], [5, 6], [7]]

    def gather(step):
        for h in range(2):
            for d in range(2):
                if step == 4 and d != h:
                    continue
                y_copy(step, d, h).wait()
                if step < 3 or (step == 3 and d == h):
                    y_copy(step + 1, d, h).start()

    def product(step):
        slots = groups[step]

        def tile(t, carry):
            total = None
            for k in range(4):
                if step == 0:
                    rows = amp_ref[k]
                elif step == 4:
                    rows = gath[4, k, k // 2]
                else:
                    rows = gath[step, k].reshape(128, 256)
                term = jnp.dot(rows, tiles[pick[k * 8 + t]], preferred_element_type=jnp.float32)
                total = term if total is None else total + term
            total = total.reshape(len(slots), NX, 2, 8, 256)
            for i, slot in enumerate(slots):
                for xx in range(NX):
                    for cc in range(2):
                        part[slot, cc, xx, t] = total[i, xx, cc]
            return carry

        lax.fori_loop(0, 8, tile, 0)
        for slot in slots:
            c_copy(slot).start()

    def join(step):
        for slot in groups[step]:
            c_copy(slot).wait()

            def add(o, carry):
                xx = lax.rem(x + o, NX)
                part[slot, core, xx] = part[slot, core, xx] + mate[slot, xx]
                return carry

            lax.fori_loop(0, NX, add, 0)
            for i in range(4):
                x_copy(slot, i).start()

    def pass_on(step):
        for slot in groups[step]:
            for i, to, half in ((0, xp, low), (1, xm, high)):
                x_copy(slot, i).wait()
                part[slot, core, to, half] = part[slot, core, to, half] + relay[slot, i]
                x_copy(slot, 4 + i).start()

    def across(step):
        for slot in groups[step]:
            for i in range(2, 6):
                x_copy(slot, i).wait()
            red[slot] = part[slot, core, x] + near[slot, 0] + near[slot, 1]
            if slot < 7:
                @pl.when(ahead(slot) == 4)
                def _():
                    z_copy(slot, 0, low).start()
                    z_copy(slot, 1, high).start()
            else:
                @pl.when(ahead(slot) != 0)
                def _():
                    last_copy(ahead(slot) - 1).start()

    def hop(step, n):
        for slot in groups[step]:
            for d, at, first in ((0, 5 - n, low), (1, 3 + n, high)):
                half = first if n == 2 else whole

                @pl.when(ahead(slot) == at)
                def _():
                    z_copy(slot, d, half).wait_recv()
                    red[slot, half] = red[slot, half] + fromz[slot, d, half]
                    z_copy(slot, d, whole).start()

    product(0)
    gather(1)
    join(0)
    product(1)
    pass_on(0)
    gather(2)
    join(1)
    across(0)
    product(2)
    pass_on(1)
    hop(0, 2)
    gather(3)
    join(2)
    across(1)
    hop(0, 3)
    product(3)
    pass_on(2)
    hop(1, 2)
    hop(0, 4)
    gather(4)
    join(3)
    across(2)
    hop(1, 3)
    product(4)
    pass_on(3)
    hop(2, 2)
    hop(1, 4)
    join(4)
    across(3)
    hop(2, 3)
    pass_on(4)
    hop(3, 2)
    hop(2, 4)
    across(4)
    hop(3, 3)
    hop(3, 4)

    for slot in range(7):
        p = ahead(slot)

        @pl.when(p == 0)
        def _():
            z_copy(slot, 0, whole).wait_recv()
            z_copy(slot, 1, whole).wait_recv()
            out_ref[...] = red[slot] + fromz[slot, 0] + fromz[slot, 1]

        @pl.when(p == 4)
        def _():
            z_copy(slot, 0, low).wait_send()
            z_copy(slot, 1, high).wait_send()

        @pl.when((p > 0) & (p < 4))
        def _():
            z_copy(slot, 0, whole).wait_send()

        @pl.when(p > 4)
        def _():
            z_copy(slot, 1, whole).wait_send()

    @pl.when(ahead(7) == 0)
    def _():
        total = red[7]
        for o in range(7):
            last_copy(o).wait_recv()
            total = total + last[o]
        out_ref[...] = total

    @pl.when(ahead(7) != 0)
    def _():
        last_copy(ahead(7) - 1).wait_send()


def body(amplitudes, integrals, screen, owner_map):
    amp = jnp.transpose(amplitudes, (1, 0, 2))
    tiles = integrals.reshape(24, 256, 256)
    f32 = jnp.float32
    dma = pltpu.SemaphoreType.DMA
    out = pl.pallas_call(
        kernel,
        out_shape=jax.ShapeDtypeStruct((8, 8, 256), f32),
        in_specs=[
            pl.BlockSpec(memory_space=pltpu.SMEM),
            pl.BlockSpec(memory_space=pltpu.SMEM),
            pl.BlockSpec(memory_space=pltpu.VMEM),
            pl.BlockSpec(memory_space=pl.ANY),
        ],
        out_specs=pl.BlockSpec(memory_space=pltpu.VMEM),
        scratch_shapes=[
            pltpu.VMEM((25, 256, 256), jnp.bfloat16),
            pltpu.SMEM((32,), jnp.int32),
            pltpu.VMEM((5, 4, 2, 64, 256), jnp.bfloat16),
            pltpu.VMEM((8, 2, NX, 8, 8, 256), f32),
            pltpu.VMEM((8, NX, 8, 8, 256), f32),
            pltpu.VMEM((8, 2, 4, 8, 256), f32),
            pltpu.VMEM((8, 2, 8, 8, 256), f32),
            pltpu.VMEM((8, 8, 8, 256), f32),
            pltpu.VMEM((7, 2, 8, 8, 256), f32),
            pltpu.VMEM((7, 8, 8, 256), f32),
            dma(()),
            dma((5, 2, 2)), dma((5, 2, 2)),
            dma((8,)), dma((8,)),
            dma((8, 6)), dma((8, 6)),
            dma((7, 2)), dma((7, 2)),
            dma(()), dma((7,)),
        ],
        compiler_params=pltpu.CompilerParams(collective_id=0, has_side_effects=True),
    )(screen, owner_map, amp, tiles)
    return jnp.transpose(out, (1, 0, 2))


def solution(mesh):
    return jax.shard_map(
        body,
        mesh=mesh,
        in_specs=(
            P("col", "row", None),
            P("row", "col", None, None),
            P("row", "col"),
            P("col", None),
        ),
        out_specs=P("row", "col", None),
        check_vma=False,
    )
```

```python
import jax
import jax.numpy as jnp
from jax import lax
from jax.experimental import pallas as pl
from jax.experimental.pallas import tpu as pltpu
from jax.sharding import PartitionSpec as P

MESH = pl.DeviceIdType.MESH
NX, NZ, NY = 4, 8, 8


def kernel(screen_ref, owner_ref, amp_ref, integrals_ref, out_ref,
           tiles, pick, gath, part, mate, fromx, red, fromz,
           load_sem, y_send, y_recv, c_send, c_recv, x_send, x_recv, z_send, z_recv):
    row, y = lax.axis_index("row"), lax.axis_index("col")
    core = lax.rem(row, 2)
    x = lax.rem(row // 2, NX)
    z = row // (2 * NX)

    def dev(zz, xx, cc):
        return ((zz * NX + xx) * 2 + cc, y)

    right = (row, lax.rem(y + 1, NY))
    left = (row, lax.rem(y + NY - 1, NY))

    load = pltpu.make_async_copy(integrals_ref, tiles.at[pl.ds(0, 24)], load_sem)
    load.start()

    barrier = pltpu.get_barrier_semaphore()
    peers = [right, left, dev(z, x, 1 - core)]
    peers += [dev(z, lax.rem(x + o, NX), core) for o in range(1, NX)]
    peers += [dev(lax.rem(z + o, NZ), x, core) for o in range(1, NZ)]
    for peer in peers:
        pl.semaphore_signal(barrier, inc=1, device_id=peer, device_id_type=MESH)
    pl.semaphore_wait(barrier, len(peers))

    def y_copy(step, d, h):
        k = pl.ds(2 * h, 2)
        src = amp_ref.at[k] if step == 1 else gath.at[step - 1, k, d]
        return pltpu.make_async_remote_copy(
            src_ref=src, dst_ref=gath.at[step, k, d],
            send_sem=y_send.at[step, d, h], recv_sem=y_recv.at[step, d, h],
            device_id=right if d == 0 else left, device_id_type=MESH)

    def pieces(slot):
        return [(slot, pl.ds(0, 8))] if slot < 7 else [(7, pl.ds(0, 4)), (8, pl.ds(4, 4))]

    def c_copy(slot, i, ts):
        return pltpu.make_async_remote_copy(
            src_ref=part.at[slot, 1 - core, :, ts], dst_ref=mate.at[slot, :, ts],
            send_sem=c_send.at[i], recv_sem=c_recv.at[i],
            device_id=dev(z, x, 1 - core), device_id_type=MESH)

    def x_copy(slot, o, i, ts):
        xx = lax.rem(x + o, NX)
        return pltpu.make_async_remote_copy(
            src_ref=part.at[slot, core, xx, ts], dst_ref=fromx.at[slot, o - 1, ts],
            send_sem=x_send.at[i, o - 1], recv_sem=x_recv.at[i, o - 1],
            device_id=dev(z, xx, core), device_id_type=MESH)

    def block_of(slot):
        if slot == 0:
            return y
        s = (slot + 1) // 2
        return lax.rem(y + NY - s, NY) if slot % 2 == 1 else lax.rem(y + s, NY)

    def z_copy(slot, i, ts):
        return pltpu.make_async_remote_copy(
            src_ref=red.at[slot, ts], dst_ref=fromz.at[z, ts],
            send_sem=z_send.at[i], recv_sem=z_recv.at[z, max(i - 7, 0)],
            device_id=dev(block_of(slot), x, core), device_id_type=MESH)

    for h in range(2):
        for d in range(2):
            y_copy(1, d, h).start()

    tiles[24] = jnp.zeros((256, 256), jnp.bfloat16)
    for t in range(8):
        label = jnp.int32(0)
        for g in range(8):
            label = jnp.where(owner_ref[0, g] == t, g, label)
        for k in range(4):
            at = jnp.int32(24)
            for l in range(6):
                at = jnp.where(screen_ref[k, l] == label, k * 6 + l, at)
            pick[k * 8 + t] = at
    load.wait()

    groups = [[0], [1, 2], [3, 4], [5, 6], [7]]

    def gather(step):
        for h in range(2):
            for d in range(2):
                if step == 4 and d != h:
                    continue
                y_copy(step, d, h).wait()
                if step < 3 or (step == 3 and d == h):
                    y_copy(step + 1, d, h).start()

    def product(step):
        slots = groups[step]

        def tile(t, carry):
            total = None
            for k in range(4):
                if step == 0:
                    rows = amp_ref[k]
                elif step == 4:
                    rows = gath[4, k, k // 2]
                else:
                    rows = gath[step, k].reshape(128, 256)
                term = jnp.dot(rows, tiles[pick[k * 8 + t]], preferred_element_type=jnp.float32)
                total = term if total is None else total + term
            total = total.reshape(len(slots), NX, 2, 8, 256)
            for i, slot in enumerate(slots):
                for xx in range(NX):
                    for cc in range(2):
                        part[slot, cc, xx, t] = total[i, xx, cc]
            return carry

        for n in range(len(pieces(slots[-1]))):
            size = 8 // len(pieces(slots[-1]))
            lax.fori_loop(n * size, (n + 1) * size, tile, 0)
            for slot in slots:
                c_copy(slot, *pieces(slot)[n]).start()

    def join(step):
        for slot in groups[step]:
            for i, ts in pieces(slot):
                c_copy(slot, i, ts).wait()
                for o in (2, 1, 3, 0):
                    xx = lax.rem(x + o, NX)
                    part[slot, core, xx, ts] = part[slot, core, xx, ts] + mate[slot, xx, ts]
                    if o:
                        x_copy(slot, o, i, ts).start()

    def across(step):
        for slot in groups[step]:
            block = block_of(slot)
            for i, ts in pieces(slot):
                for o in range(1, NX):
                    x_copy(slot, o, i, ts).wait()
                total = part[slot, core, x, ts]
                for o in range(1, NX):
                    total = total + fromx[slot, o - 1, ts]

                @pl.when(block == z)
                def _():
                    fromz[z, ts] = total

                @pl.when(block != z)
                def _():
                    red[slot, ts] = total
                    z_copy(slot, i, ts).start()

    product(0)
    for step in range(1, 5):
        gather(step)
        product(step)
        join(step - 1)
        if step >= 2:
            across(step - 2)
    join(4)
    across(3)
    across(4)

    for slot in range(8):
        @pl.when(block_of(slot) != z)
        def _():
            for i, ts in pieces(slot):
                z_copy(slot, i, ts).wait_send()

    def arrived(slot):
        for o in range(1, NZ):
            zz = lax.rem(z + o, NZ)
            for i, ts in pieces(slot):
                pltpu.make_async_remote_copy(
                    src_ref=red.at[0, ts], dst_ref=fromz.at[zz, ts],
                    send_sem=z_send.at[0], recv_sem=z_recv.at[zz, max(i - 7, 0)],
                    device_id=dev(zz, x, core), device_id_type=MESH).wait_recv()

    @pl.when(block_of(7) != z)
    def _():
        arrived(0)

    @pl.when(block_of(7) == z)
    def _():
        arrived(7)

    total = fromz[0]
    for zz in range(1, NZ):
        total = total + fromz[zz]
    out_ref[...] = total


def body(amplitudes, integrals, screen, owner_map):
    amp = jnp.transpose(amplitudes, (1, 0, 2))
    tiles = integrals.reshape(24, 256, 256)
    f32 = jnp.float32
    dma = pltpu.SemaphoreType.DMA
    out = pl.pallas_call(
        kernel,
        out_shape=jax.ShapeDtypeStruct((8, 8, 256), f32),
        in_specs=[
            pl.BlockSpec(memory_space=pltpu.SMEM),
            pl.BlockSpec(memory_space=pltpu.SMEM),
            pl.BlockSpec(memory_space=pltpu.VMEM),
            pl.BlockSpec(memory_space=pl.ANY),
        ],
        out_specs=pl.BlockSpec(memory_space=pltpu.VMEM),
        scratch_shapes=[
            pltpu.VMEM((25, 256, 256), jnp.bfloat16),
            pltpu.SMEM((32,), jnp.int32),
            pltpu.VMEM((5, 4, 2, 64, 256), jnp.bfloat16),
            pltpu.VMEM((8, 2, NX, 8, 8, 256), f32),
            pltpu.VMEM((8, NX, 8, 8, 256), f32),
            pltpu.VMEM((8, NX - 1, 8, 8, 256), f32),
            pltpu.VMEM((8, 8, 8, 256), f32),
            pltpu.VMEM((8, 8, 8, 256), f32),
            dma(()),
            dma((5, 2, 2)), dma((5, 2, 2)),
            dma((9,)), dma((9,)),
            dma((9, 3)), dma((9, 3)),
            dma((9,)), dma((8, 2)),
        ],
        compiler_params=pltpu.CompilerParams(collective_id=0, has_side_effects=True),
    )(screen, owner_map, amp, tiles)
    return jnp.transpose(out, (1, 0, 2))


def solution(mesh):
    return jax.shard_map(
        body,
        mesh=mesh,
        in_specs=(
            P("col", "row", None),
            P("row", "col", None, None),
            P("row", "col"),
            P("col", None),
        ),
        out_specs=P("row", "col", None),
        check_vma=False,
    )
```
